32 devices in a mesh: seq: 4 (over z), dp: 8 (over y, x, core).
Axes of the slice: x: 2, y: 2, z: 4, core: 2. Of those that a mesh axis runs over, the one named last changes fastest.
Arguments:
- stream: float32 [8, 512, 1152], P('dp', 'seq'), may hold values from -50 to 50
- stream_grad: float32 [8, 512, 1152], P('dp', 'seq'), may hold values from -6 to 6
- lengths: int32 [8, 4], P('dp'), may hold values from 1 to 384, 512 in all within a row
- w_qkv: bfloat16 [1152, 1536], P(('seq', 'dp')), may hold values from -0.1875 to 0.1875
- w_out: bfloat16 [1024, 1152], P(('seq', 'dp')), may hold values from -0.1875 to 0.1875
- w_gate: bfloat16 [6912, 1152], P(('seq', 'dp')), may hold values from -0.1875 to 0.1875
- w_up: bfloat16 [6912, 1152], P(('seq', 'dp')), may hold values from -0.1875 to 0.1875
- w_down: bfloat16 [6912, 1152], P(('seq', 'dp')), may hold values from -0.078125 to 0.078125
- g_attn_in: float32 [1152], replicated, may hold values from 0.25 to 1.75
- g_query: float32 [256], replicated, may hold values from 0.25 to 1.75
- g_key: float32 [256], replicated, may hold values from 0.25 to 1.75
- g_attn_out: float32 [1152], replicated, may hold values from 0.25 to 1.75
- g_ffn_in: float32 [1152], replicated, may hold values from 0.25 to 1.75
- g_ffn_out: float32 [1152], replicated, may hold values from 0.25 to 1.75
Outputs:
- result: float32 [8, 512, 1152], P('dp', 'seq')
- input_grad: float32 [8, 512, 1152], P('dp', 'seq')
- grad_w_qkv: float32 [1152, 1536], P(('seq', 'dp'))
- grad_w_out: float32 [1024, 1152], P(('seq', 'dp'))
- grad_w_gate: float32 [6912, 1152], P(('seq', 'dp'))
- grad_w_up: float32 [6912, 1152], P(('seq', 'dp'))
- grad_w_down: float32 [6912, 1152], P(('seq', 'dp'))
- grad_g_attn_in: float32 [1152], P(('seq', 'dp'))
- grad_g_query: float32 [256], P(('seq', 'dp'))
- grad_g_key: float32 [256], P(('seq', 'dp'))
- grad_g_attn_out: float32 [1152], P(('seq', 'dp'))
- grad_g_ffn_in: float32 [1152], P(('seq', 'dp'))
- grad_g_ffn_out: float32 [1152], P(('seq', 'dp'))
The draws below stay inside these ranges and needn't reach their ends.
Inputs may be any that keep to these rules, and one draw needn't show every extreme that they name: Each row lists the lengths of the 4 sequences packed in order into one group; they sum to 512.
All inputs are finite; a program needn't handle non-finite values.
Results may differ from the reference program's by a relative error of at most 0.015.
Values may be sent and summed in bfloat16 or wider, within the bound.
A program may use at most 128 MiB of HBM per device.

```python
import math
import jax
import jax.numpy as jnp
import numpy as np
from jax import lax

D = 1152
HEADS = 4
HEAD_DIM = 256
FF = 6912
WINDOW = 512
SEQS = 4
SEQ_TOKENS = 512
GROUPS = 8
QUERY_WIDTH = 1024
QKV_WIDTH = 1536


def draw_stream(key, part):
    first, second, third = jax.random.split(key, 3)
    shape = (GROUPS, SEQ_TOKENS, D)
    base = jax.random.truncated_normal(first, -5.0, 5.0, shape, jnp.float32)
    row_scale = jnp.exp(jax.random.uniform(second, (GROUPS, SEQ_TOKENS, 1), jnp.float32, -1.15, 1.15))
    col_scale = jnp.exp(jax.random.uniform(third, (1, 1, D), jnp.float32, -1.15, 1.15))
    return base * row_scale * col_scale


def shard_levels(rng, dims, cuts, smallest, largest):
    level, own = 1.0, jax.random.fold_in(rng, 6)
    for axis_at, shards_of in cuts:
        heights = jnp.exp(jax.random.uniform(jax.random.fold_in(own, axis_at), (shards_of,), jnp.float32, smallest / len(cuts), largest / len(cuts)))
        level = level * jnp.repeat(heights, dims[axis_at] // shards_of).reshape([-1 if axis == axis_at else 1 for axis in range(len(dims))])
    return level


def length_profile(number_of, total, most, slope):
    loads = [(1 << 20) // math.isqrt(standing ** slope) + 1 for standing in range(2, number_of + 1)]
    rest, given = total - most - (number_of - 1), [1] * (number_of - 1)
    while rest > 0:
        movable = [i for i in range(number_of - 1) if given[i] < most]
        mass, budget = sum([loads[i] for i in movable]), rest
        for i in movable:
            extra = min(most - given[i], max(1, budget * loads[i] // mass), rest)
            given[i] = given[i] + extra
            rest = rest - extra
    return np.array([most] + given)


def ragged_sizes(key, number_of, total, most, slope):
    if number_of == 2:
        one = jax.random.randint(key, (), max(1, total - most), min(most, total - 1) + 1)
        return jnp.stack([one, total - one])
    sizes = jnp.asarray(length_profile(number_of, total, most, slope), jnp.int32)
    couples = (number_of - 1) // 2
    donor, sink = sizes[1:1 + 2 * couples:2], sizes[2:2 + 2 * couples:2]
    room = jnp.minimum(donor - 1, most - sink)
    passed = jax.random.randint(jax.random.fold_in(key, 1), (couples,), 0, 1 << 20) % (room + 1)
    sizes = sizes.at[1:1 + 2 * couples:2].set(donor - passed).at[2:2 + 2 * couples:2].set(sink + passed)
    return sizes[jax.random.permutation(jax.random.fold_in(key, 2), number_of)]


def gaussian(rng, extent, width, reach, cuts=(), kind=jnp.bfloat16):
    factor_of = shard_levels(rng, extent, cuts, -0.22, 0.18) if cuts else 1.0
    values = jax.random.normal(rng, extent, jnp.float32) * width * factor_of
    return jnp.minimum(jnp.maximum(values, -reach), reach).astype(kind)


def setup_inputs(seed: int = 0) -> dict:
    streams_of = jax.random.split(jax.random.key(seed), 15)
    stream = draw_stream(jax.random.fold_in(streams_of[14], 71), 0)
    stream_grad = gaussian(streams_of[1], (GROUPS, SEQ_TOKENS, D), 1.0, 6.0, ((0, 8), (1, 4)), jnp.float32)
    lengths = jax.vmap(lambda own: ragged_sizes(own, SEQS, SEQ_TOKENS, SEQ_TOKENS * 3 // 4, 2))(jax.random.split(streams_of[2], GROUPS)).reshape((GROUPS, SEQS)).astype(jnp.int32)
    w_qkv = gaussian(streams_of[3], (D, QKV_WIDTH), D ** -0.5, 0.1875, ((0, 32),))
    w_out = gaussian(streams_of[4], (QUERY_WIDTH, D), QUERY_WIDTH ** -0.5, 0.1875, ((0, 32),))
    w_gate = gaussian(streams_of[5], (FF, D), D ** -0.5, 0.1875, ((0, 32),))
    w_up = gaussian(streams_of[6], (FF, D), D ** -0.5, 0.1875, ((0, 32),))
    w_down = gaussian(streams_of[7], (FF, D), FF ** -0.5, 0.078125, ((0, 32),))
    g_attn_in = jnp.clip(1.0 + 0.15 * jax.random.normal(streams_of[8], (D,), jnp.float32), 0.25, 1.75)
    g_query = jnp.clip(1.0 + 0.15 * jax.random.normal(streams_of[9], (HEAD_DIM,), jnp.float32), 0.25, 1.75)
    g_key = jnp.clip(1.0 + 0.15 * jax.random.normal(streams_of[10], (HEAD_DIM,), jnp.float32), 0.25, 1.75)
    g_attn_out = jnp.clip(1.0 + 0.15 * jax.random.normal(streams_of[11], (D,), jnp.float32), 0.25, 1.75)
    g_ffn_in = jnp.clip(1.0 + 0.15 * jax.random.normal(streams_of[12], (D,), jnp.float32), 0.25, 1.75)
    g_ffn_out = jnp.clip(1.0 + 0.15 * jax.random.normal(streams_of[13], (D,), jnp.float32), 0.25, 1.75)
    return {"stream": stream, "stream_grad": stream_grad, "lengths": lengths, "w_qkv": w_qkv, "w_out": w_out, "w_gate": w_gate, "w_up": w_up, "w_down": w_down, "g_attn_in": g_attn_in, "g_query": g_query, "g_key": g_key, "g_attn_out": g_attn_out, "g_ffn_in": g_ffn_in, "g_ffn_out": g_ffn_out}


EPSILON = 1e-06
GELU_SLOPE = math.sqrt(2.0 / math.pi)
GELU_CUBIC = 0.044715

def inv_root(vector):
    return lax.rsqrt(lax.optimization_barrier(jnp.mean(vector * vector, axis=-1, keepdims=True)) + EPSILON)

def norm_back(grad, unit_part, root_part, gain):
    scaled = grad * gain
    return root_part * (scaled - unit_part * lax.optimization_barrier(jnp.mean(scaled * unit_part, axis=-1, keepdims=True)))

def gelu_pair(gate):
    inner = jnp.tanh(GELU_SLOPE * (gate + GELU_CUBIC * gate * gate * gate))
    gelu_value = 0.5 * gate * (1.0 + inner)
    gelu_slope = 0.5 * (1.0 + inner) + 0.5 * gate * (1.0 - inner * inner) * GELU_SLOPE * (1.0 + 3.0 * GELU_CUBIC * gate * gate)
    return (gelu_value, gelu_slope)

def turn_half(vector):
    half = vector.shape[-1] // 2
    return jnp.concatenate([-vector[..., half:], vector[..., :half]], axis=-1)

def seq_begin(index, starts):
    return lax.optimization_barrier(jnp.max(jnp.where(starts[None, :] <= index[:, None], starts[None, :], 0), axis=1)).astype(jnp.int32)

def rope_tables(position, head):
    freq = jnp.exp(-math.log(10000.0) * jnp.arange(head // 2, dtype=jnp.float32) * (2.0 / head))
    angle = position[:, None] * freq[None, :]
    angle = jnp.concatenate([angle, angle], axis=1)
    return (jnp.cos(angle), jnp.sin(angle))

def dot32(left, right):
    return jnp.dot(left, right, preferred_element_type=jnp.float32)

def group_pass(rows_in, rows_grad, lens, w_qkv, w_out, w_gate, w_up, w_down, g_attn_in, g_query, g_key, g_attn_out, g_ffn_in, g_ffn_out):
    count = rows_in.shape[0]
    qwidth = HEADS * HEAD_DIM
    index = jnp.arange(count, dtype=jnp.int32)
    starts = (jnp.cumsum(lens) - lens).astype(jnp.int32)
    begin = seq_begin(index, starts)
    cos_t, sin_t = rope_tables((index - begin).astype(jnp.float32), HEAD_DIM)
    mask = (begin[:, None] == begin[None, :]) & (index[None, :] <= index[:, None]) & (index[:, None] - index[None, :] < WINDOW)
    full_mask = mask[:, None, :]
    scale = 1.0 / math.sqrt(HEAD_DIM)
    root_attn = inv_root(rows_in)
    unit_attn = rows_in * root_attn
    attn_input = (unit_attn * g_attn_in).astype(jnp.bfloat16)
    projected = dot32(attn_input, w_qkv)
    query = projected[:, :qwidth].reshape(count, HEADS, HEAD_DIM)
    key_raw = projected[:, qwidth:qwidth + HEAD_DIM]
    value_raw = projected[:, qwidth + HEAD_DIM:]
    root_query = inv_root(query)
    unit_query = query * root_query
    query_norm = unit_query * g_query
    root_key = inv_root(key_raw)
    unit_key = key_raw * root_key
    key_norm = unit_key * g_key
    query_rot = query_norm * cos_t[:, None, :] + turn_half(query_norm) * sin_t[:, None, :]
    key_rot = key_norm * cos_t + turn_half(key_norm) * sin_t
    query_b = query_rot.astype(jnp.bfloat16)
    key_b = key_rot.astype(jnp.bfloat16)
    value_b = value_raw.astype(jnp.bfloat16)
    scores = jnp.einsum('qhd,kd->qhk', query_b.astype(jnp.float32), key_b.astype(jnp.float32)) * scale
    logsum = jnp.log(lax.optimization_barrier(jnp.sum(jnp.where(full_mask, jnp.exp(scores), 0.0), axis=-1)))
    probs = jnp.where(full_mask, jnp.exp(scores - logsum[..., None]), 0.0)
    probs_b = probs.astype(jnp.bfloat16)
    mixed = jnp.einsum('qhk,kd->qhd', probs_b.astype(jnp.float32), value_b.astype(jnp.float32))
    mixed_b = mixed.reshape(count, qwidth).astype(jnp.bfloat16)
    attn_out = dot32(mixed_b, w_out)
    root_post = inv_root(attn_out)
    unit_post = attn_out * root_post
    hidden_in = rows_in + unit_post * g_attn_out
    root_ffn = inv_root(hidden_in)
    unit_ffn = hidden_in * root_ffn
    ffn_input = (unit_ffn * g_ffn_in).astype(jnp.bfloat16)
    gate = dot32(ffn_input, w_gate.T)
    up_part = dot32(ffn_input, w_up.T)
    gelu_value, gelu_slope = gelu_pair(gate)
    hidden = (gelu_value * up_part).astype(jnp.bfloat16)
    ffn_out = dot32(hidden, w_down)
    root_out = inv_root(ffn_out)
    unit_out = ffn_out * root_out
    result = hidden_in + unit_out * g_ffn_out
    grad_g_ffn_out = lax.optimization_barrier(jnp.sum(rows_grad * unit_out, axis=0))
    ffn_grad_b = norm_back(rows_grad, unit_out, root_out, g_ffn_out).astype(jnp.bfloat16)
    hidden_grad = dot32(ffn_grad_b, w_down.T)
    dgate_b = (hidden_grad * up_part * gelu_slope).astype(jnp.bfloat16)
    dup_b = (hidden_grad * gelu_value).astype(jnp.bfloat16)
    ffn_in_grad = dot32(dgate_b, w_gate) + dot32(dup_b, w_up)
    grad_w_gate = dot32(dgate_b.T, ffn_input)
    grad_w_up = dot32(dup_b.T, ffn_input)
    grad_w_down = dot32(hidden.T, ffn_grad_b)
    grad_g_ffn_in = lax.optimization_barrier(jnp.sum(ffn_in_grad * unit_ffn, axis=0))
    hidden_grad_in = rows_grad + norm_back(ffn_in_grad, unit_ffn, root_ffn, g_ffn_in)
    grad_g_attn_out = lax.optimization_barrier(jnp.sum(hidden_grad_in * unit_post, axis=0))
    attn_grad_b = norm_back(hidden_grad_in, unit_post, root_post, g_attn_out).astype(jnp.bfloat16)
    mixed_grad_b = dot32(attn_grad_b, w_out.T).astype(jnp.bfloat16)
    grad_w_out = dot32(mixed_b.T, attn_grad_b)
    mixed_grad3 = mixed_grad_b.reshape(count, HEADS, HEAD_DIM).astype(jnp.float32)
    delta = lax.optimization_barrier(jnp.sum(mixed_grad3 * mixed_b.reshape(count, HEADS, HEAD_DIM).astype(jnp.float32), axis=-1))
    value_grad = jnp.einsum('qhk,qhd->kd', probs_b.astype(jnp.float32), mixed_grad3)
    prob_grad = jnp.einsum('qhd,kd->qhk', mixed_grad3, value_b.astype(jnp.float32))
    score_grad_b = (probs * (prob_grad - delta[..., None])).astype(jnp.bfloat16)
    query_rot_grad = jnp.einsum('qhk,kd->qhd', score_grad_b.astype(jnp.float32), key_b.astype(jnp.float32)) * scale
    key_rot_grad = jnp.einsum('qhk,qhd->kd', score_grad_b.astype(jnp.float32), query_b.astype(jnp.float32)) * scale
    query_norm_grad = query_rot_grad * cos_t[:, None, :] - turn_half(query_rot_grad * sin_t[:, None, :])
    key_norm_grad = key_rot_grad * cos_t - turn_half(key_rot_grad * sin_t)
    grad_g_query = lax.optimization_barrier(jnp.sum(query_norm_grad * unit_query, axis=(0, 1)))
    grad_g_key = lax.optimization_barrier(jnp.sum(key_norm_grad * unit_key, axis=0))
    query_grad = norm_back(query_norm_grad, unit_query, root_query, g_query)
    key_grad = norm_back(key_norm_grad, unit_key, root_key, g_key)
    qkv_grad_b = jnp.concatenate([query_grad.reshape(count, qwidth), key_grad, value_grad], axis=1).astype(jnp.bfloat16)
    attn_in_grad = dot32(qkv_grad_b, w_qkv.T)
    grad_w_qkv = dot32(attn_input.T, qkv_grad_b)
    grad_g_attn_in = lax.optimization_barrier(jnp.sum(attn_in_grad * unit_attn, axis=0))
    input_grad = hidden_grad_in + norm_back(attn_in_grad, unit_attn, root_attn, g_attn_in)
    gains = jnp.stack([grad_g_attn_in, grad_g_attn_out, grad_g_ffn_in, grad_g_ffn_out])
    head_gains = jnp.stack([grad_g_query, grad_g_key])
    return ((result, input_grad), (grad_w_qkv, grad_w_out, grad_w_gate, grad_w_up, grad_w_down, gains, head_gains))

def reference(stream, stream_grad, lengths, w_qkv, w_out, w_gate, w_up, w_down, g_attn_in, g_query, g_key, g_attn_out, g_ffn_in, g_ffn_out):

    def step(totals, inputs):
        rows_in, rows_grad, lens = inputs
        outputs, grads = group_pass(rows_in, rows_grad, lens, w_qkv, w_out, w_gate, w_up, w_down, g_attn_in, g_query, g_key, g_attn_out, g_ffn_in, g_ffn_out)
        totals = tuple((first + second for first, second in zip(totals, grads)))
        return (totals, outputs)
    init = (jnp.zeros((D, (HEADS + 2) * HEAD_DIM), jnp.float32), jnp.zeros((HEADS * HEAD_DIM, D), jnp.float32), jnp.zeros((FF, D), jnp.float32), jnp.zeros((FF, D), jnp.float32), jnp.zeros((FF, D), jnp.float32), jnp.zeros((4, D), jnp.float32), jnp.zeros((2, HEAD_DIM), jnp.float32))
    totals, outputs = lax.scan(step, init, (stream, stream_grad, lengths))
    return (outputs[0], outputs[1], totals[0], totals[1], totals[2], totals[3], totals[4], totals[5][0], totals[6][0], totals[6][1], totals[5][1], totals[5][2], totals[5][3])
```

```python
import math

import jax
import jax.numpy as jnp
from jax import lax
from jax.sharding import PartitionSpec as P

HEADS = 4
HEAD_DIM = 256
WINDOW = 512


EPSILON = 1e-06
GELU_SLOPE = math.sqrt(2.0 / math.pi)
GELU_CUBIC = 0.044715


def bits_of(count):
    bits = []
    bit = 1
    while bit < count:
        bits.append(bit)
        bit *= 2
    return bits


def swapped(value, axis, bit):
    length = lax.axis_size(axis)
    return lax.ppermute(value, axis, [(i, i ^ bit) for i in range(length)])


def mine_first(value, axis, bit, at):
    return jnp.concatenate([value, swapped(value, axis, bit)], axis=at)


def keep_half(value, axis, bit, at):
    own = lax.slice_in_dim(value, 0, 1, axis=at)
    other = lax.slice_in_dim(value, 1, 2, axis=at).astype(jnp.bfloat16)
    return own.astype(jnp.float32) + swapped(other, axis, bit).astype(jnp.float32)


def gather_xor(value, stages):
    value = value.reshape((1,) * len(stages) + value.shape)
    for axis, bit, at in stages:
        value = mine_first(value, axis, bit, at)
    return value


def scatter_xor(value, stages):
    for axis, bit, at in stages:
        value = keep_half(value, axis, bit, at)
    return value.reshape(value.shape[len(stages) :])


def ordered_pair(value, axis, bit, at):
    other = swapped(value, axis, bit)
    high = (lax.axis_index(axis) & bit) != 0
    return jnp.concatenate(
        [jnp.where(high, other, value), jnp.where(high, value, other)], axis=at
    )


def gather_ordered(value, stages):
    value = value.reshape((1,) * len(stages) + value.shape)
    for axis, bit, at in stages:
        value = ordered_pair(value, axis, bit, at)
    return value


def scatter_ordered(value, stages, dtype):
    for axis, bit, at in stages:
        high = (lax.axis_index(axis) & bit) != 0
        low_half = lax.slice_in_dim(value, 0, 1, axis=at)
        high_half = lax.slice_in_dim(value, 1, 2, axis=at)
        own = jnp.where(high, high_half, low_half).astype(jnp.float32)
        sent = jnp.where(high, low_half, high_half).astype(dtype)
        value = own + swapped(sent, axis, bit).astype(jnp.float32)
    return value.reshape(value.shape[len(stages) :])


def inv_root(vector):
    return lax.rsqrt(jnp.mean(vector * vector, axis=-1, keepdims=True) + EPSILON)


def norm_back(grad, unit_part, root_part, gain):
    scaled = grad * gain
    return root_part * (scaled - unit_part * jnp.mean(scaled * unit_part, axis=-1, keepdims=True))


def gelu_pair(gate):
    inner = jnp.tanh(GELU_SLOPE * (gate + GELU_CUBIC * gate * gate * gate))
    gelu_value = 0.5 * gate * (1.0 + inner)
    gelu_slope = 0.5 * (1.0 + inner) + 0.5 * gate * (1.0 - inner * inner) * GELU_SLOPE * (
        1.0 + 3.0 * GELU_CUBIC * gate * gate
    )
    return (gelu_value, gelu_slope)


def turn_half(vector):
    half = vector.shape[-1] // 2
    return jnp.concatenate([-vector[..., half:], vector[..., :half]], axis=-1)


def seq_begin(index, starts):
    return jnp.max(jnp.where(starts[None, :] <= index[:, None], starts[None, :], 0), axis=1)


def rope_tables(position, head):
    freq = jnp.exp(-math.log(10000.0) * jnp.arange(head // 2, dtype=jnp.float32) * (2.0 / head))
    angle = position[:, None] * freq[None, :]
    angle = jnp.concatenate([angle, angle], axis=1)
    return (jnp.cos(angle), jnp.sin(angle))


def dot32(left, right):
    return jnp.dot(left, right, preferred_element_type=jnp.float32)


def contract_rows(left, right):
    return lax.dot_general(
        left, right, (((0,), (0,)), ((), ())), preferred_element_type=jnp.float32
    )


def contract_cols(left, right):
    return lax.dot_general(
        left, right, (((1,), (1,)), ((), ())), preferred_element_type=jnp.float32
    )


def ffn_forward_fold(tokens_b, pieces):
    gate_rows, up_rows, down_rows = pieces
    gate_part = contract_cols(tokens_b, gate_rows)
    up_part = contract_cols(tokens_b, up_rows)
    gelu_value, gelu_slope = gelu_pair(gate_part)
    hidden = (gelu_value * up_part).astype(jnp.bfloat16)
    out_total = dot32(hidden, down_rows)
    return (out_total, gate_part, up_part)


def ffn_backward_fold(grad_b, gate_all, up_all, pieces):
    gate_rows, up_rows, down_rows = pieces
    hidden_grad = contract_cols(grad_b, down_rows)
    gelu_value, gelu_slope = gelu_pair(gate_all)
    dgate_b = (hidden_grad * up_all * gelu_slope).astype(jnp.bfloat16)
    dup_b = (hidden_grad * gelu_value).astype(jnp.bfloat16)
    in_total = dot32(dgate_b, gate_rows) + dot32(dup_b, up_rows)
    return (in_total, dgate_b, dup_b)


def ffn_weight_terms(tokens_b, grad_b, gate_all, up_all, dgate_all, dup_all):
    gelu_value, gelu_slope = gelu_pair(gate_all)
    hidden = (gelu_value * up_all).astype(jnp.bfloat16)
    return (
        contract_rows(dgate_all, tokens_b),
        contract_rows(dup_all, tokens_b),
        contract_rows(hidden, grad_b),
    )


def local(
    stream,
    stream_grad,
    lengths,
    w_qkv,
    w_out,
    w_gate,
    w_up,
    w_down,
    g_attn_in,
    g_query,
    g_key,
    g_attn_out,
    g_ffn_in,
    g_ffn_out,
):
    rows_in = stream[0]
    rows_grad = stream_grad[0]
    lens = lengths[0]
    rows = rows_in.shape[0]
    width = rows_in.shape[1]
    qwidth = HEADS * HEAD_DIM
    seq_count = lax.axis_size("seq")
    chip_bits = [2 * bit for bit in bits_of(lax.axis_size("dp") // 2)]
    seq_bits = bits_of(seq_count)
    nseq, nchip = len(seq_bits), len(chip_bits)
    seq_stages = [("seq", bit, nseq - 1 - k) for k, bit in enumerate(seq_bits)][::-1]
    chip_stages = [("dp", bit, nseq + nchip - 1 - k) for k, bit in enumerate(chip_bits)]
    core_stage = [("dp", 1, nseq + nchip)]
    all_up = seq_stages + chip_stages + core_stage
    all_down = seq_stages + chip_stages[::-1] + core_stage
    kv_stages = seq_stages
    token_stages = seq_stages + [("dp", 1, nseq)]
    ffn_up = [("dp", bit, nchip - 1 - k) for k, bit in enumerate(chip_bits)]
    ffn_down = ffn_up[::-1]
    keys = seq_count * rows
    cut = (width // 256) * 128 + (128 if width % 256 else 0)
    scale = 1.0 / math.sqrt(HEAD_DIM)
    qkv_full = gather_ordered(w_qkv, all_up).reshape(-1, w_qkv.shape[1])
    out_full = gather_ordered(w_out, all_down).reshape(-1, w_out.shape[1])
    ffn_rows = jnp.stack([w_gate, w_up, w_down])
    left_rows, right_rows, qkv_full, out_full = lax.optimization_barrier(
        (ffn_rows[:, :, :cut], ffn_rows[:, :, cut:], qkv_full, out_full)
    )
    ffn_full = jnp.concatenate(
        [gather_xor(left_rows, ffn_up), gather_xor(right_rows, ffn_down)], axis=-1
    )
    ffn_full = ffn_full.reshape((-1,) + ffn_rows.shape)
    gate_full, up_full, down_full = (ffn_full[:, i].reshape(-1, width) for i in range(3))
    block_id = lax.axis_index("seq")
    starts = jnp.cumsum(lens) - lens
    own_index = block_id * rows + jnp.arange(rows, dtype=jnp.int32)
    key_index = (
        (block_id ^ jnp.arange(seq_count, dtype=jnp.int32))[:, None] * rows
        + jnp.arange(rows, dtype=jnp.int32)[None, :]
    ).reshape(keys)
    own_begin = seq_begin(own_index, starts)
    key_begin = seq_begin(key_index, starts)
    mask = (
        (key_begin[None, :] == own_begin[:, None])
        & (key_index[None, :] <= own_index[:, None])
        & (own_index[:, None] - key_index[None, :] < WINDOW)
    )
    full_mask = mask[:, None, :]
    cos_t, sin_t = rope_tables((own_index - own_begin).astype(jnp.float32), HEAD_DIM)
    root_attn = inv_root(rows_in)
    unit_attn = rows_in * root_attn
    attn_input = (unit_attn * g_attn_in).astype(jnp.bfloat16)
    projected = dot32(attn_input, qkv_full)
    query = projected[:, :qwidth].reshape(rows, HEADS, HEAD_DIM)
    key_raw = projected[:, qwidth : qwidth + HEAD_DIM]
    value_raw = projected[:, qwidth + HEAD_DIM :]
    root_query = inv_root(query)
    unit_query = query * root_query
    query_norm = unit_query * g_query
    root_key = inv_root(key_raw)
    unit_key = key_raw * root_key
    key_norm = unit_key * g_key
    query_rot = query_norm * cos_t[:, None, :] + turn_half(query_norm) * sin_t[:, None, :]
    key_rot = key_norm * cos_t + turn_half(key_norm) * sin_t
    query_b = query_rot.astype(jnp.bfloat16)
    kv_own = jnp.concatenate([key_rot.astype(jnp.bfloat16), value_raw.astype(jnp.bfloat16)], axis=1)
    kv_all = gather_xor(kv_own, kv_stages).reshape(keys, 2 * HEAD_DIM)
    keys_b = kv_all[:, :HEAD_DIM]
    values_b = kv_all[:, HEAD_DIM:]
    scores = jnp.einsum("rhd,kd->rhk", query_b, keys_b, preferred_element_type=jnp.float32) * scale
    logsum = jnp.log(jnp.sum(jnp.where(full_mask, jnp.exp(scores), 0.0), axis=-1))
    probs = jnp.where(full_mask, jnp.exp(scores - logsum[..., None]), 0.0)
    probs_b = probs.astype(jnp.bfloat16)
    mixed = jnp.einsum("rhk,kd->rhd", probs_b, values_b, preferred_element_type=jnp.float32)
    mixed_b = mixed.reshape(rows, qwidth).astype(jnp.bfloat16)
    attn_out = dot32(mixed_b, out_full)
    root_post = inv_root(attn_out)
    unit_post = attn_out * root_post
    hidden_in = rows_in + unit_post * g_attn_out
    root_ffn = inv_root(hidden_in)
    unit_ffn = hidden_in * root_ffn
    ffn_input = (unit_ffn * g_ffn_in).astype(jnp.bfloat16)
    slots = (2,) * len(token_stages)
    tokens_b = gather_xor(ffn_input, token_stages).reshape(-1, width)
    out_part, gate_all, up_all = ffn_forward_fold(tokens_b, (gate_full, up_full, down_full))
    ffn_out = scatter_xor(out_part.reshape(slots + (rows, width)), token_stages[::-1])
    root_out = inv_root(ffn_out)
    unit_out = ffn_out * root_out
    result = hidden_in + unit_out * g_ffn_out
    grad_g_ffn_out = jnp.sum(rows_grad * unit_out, axis=0)
    ffn_grad_b = norm_back(rows_grad, unit_out, root_out, g_ffn_out).astype(jnp.bfloat16)
    grads_b = gather_xor(ffn_grad_b, token_stages).reshape(-1, width)
    in_part, dgate_all, dup_all = ffn_backward_fold(
        grads_b, gate_all, up_all, (gate_full, up_full, down_full)
    )
    ffn_in_grad = scatter_xor(in_part.reshape(slots + (rows, width)), token_stages[::-1])
    terms = ffn_weight_terms(tokens_b, grads_b, gate_all, up_all, dgate_all, dup_all)
    chips = (2,) * nchip
    own_rows = w_gate.shape[0]

    def term_part(first, last):
        return jnp.stack(
            [term[:, first:last].reshape(chips + (own_rows, last - first)) for term in terms],
            axis=nchip,
        )

    ffn_terms = jnp.concatenate(
        [
            scatter_xor(term_part(0, cut), ffn_up),
            scatter_xor(term_part(cut, width), ffn_down),
        ],
        axis=-1,
    )
    grad_w_gate, grad_w_up, grad_w_down = ffn_terms[0], ffn_terms[1], ffn_terms[2]
    grad_g_ffn_in = jnp.sum(ffn_in_grad * unit_ffn, axis=0)
    hidden_grad_in = rows_grad + norm_back(ffn_in_grad, unit_ffn, root_ffn, g_ffn_in)
    grad_g_attn_out = jnp.sum(hidden_grad_in * unit_post, axis=0)
    attn_grad_b = norm_back(hidden_grad_in, unit_post, root_post, g_attn_out).astype(jnp.bfloat16)
    mixed_grad_b = contract_cols(attn_grad_b, out_full).astype(jnp.bfloat16)
    mixed_grad3 = mixed_grad_b.reshape(rows, HEADS, HEAD_DIM)
    delta = jnp.sum(
        mixed_grad3.astype(jnp.float32)
        * mixed_b.reshape(rows, HEADS, HEAD_DIM).astype(jnp.float32),
        axis=-1,
    )
    scores_again = (
        jnp.einsum("rhd,kd->rhk", query_b, keys_b, preferred_element_type=jnp.float32) * scale
    )
    probs_again = jnp.where(full_mask, jnp.exp(scores_again - logsum[..., None]), 0.0)
    probs_again_b = probs_again.astype(jnp.bfloat16)
    value_grad_all = jnp.einsum(
        "rhk,rhd->kd", probs_again_b, mixed_grad3, preferred_element_type=jnp.float32
    )
    prob_grad = jnp.einsum("rhd,kd->rhk", mixed_grad3, values_b, preferred_element_type=jnp.float32)
    score_grad_b = (probs_again * (prob_grad - delta[..., None])).astype(jnp.bfloat16)
    query_rot_grad = (
        jnp.einsum("rhk,kd->rhd", score_grad_b, keys_b, preferred_element_type=jnp.float32) * scale
    )
    key_grad_all = (
        jnp.einsum("rhk,rhd->kd", score_grad_b, query_b, preferred_element_type=jnp.float32) * scale
    )
    kv_grad_all = jnp.concatenate([key_grad_all, value_grad_all], axis=1)
    kv_grad = scatter_xor(
        kv_grad_all.reshape((2,) * nseq + (rows, 2 * HEAD_DIM)), kv_stages[::-1]
    )
    key_rot_grad = kv_grad[:, :HEAD_DIM]
    value_grad = kv_grad[:, HEAD_DIM:]
    query_norm_grad = query_rot_grad * cos_t[:, None, :] - turn_half(
        query_rot_grad * sin_t[:, None, :]
    )
    key_norm_grad = key_rot_grad * cos_t - turn_half(key_rot_grad * sin_t)
    grad_g_query = jnp.sum(query_norm_grad * unit_query, axis=(0, 1))
    grad_g_key = jnp.sum(key_norm_grad * unit_key, axis=0)
    query_grad = norm_back(query_norm_grad, unit_query, root_query, g_query)
    key_grad = norm_back(key_norm_grad, unit_key, root_key, g_key)
    qkv_grad_b = jnp.concatenate(
        [query_grad.reshape(rows, qwidth), key_grad, value_grad], axis=1
    ).astype(jnp.bfloat16)
    attn_in_grad = contract_cols(qkv_grad_b, qkv_full)
    grad_g_attn_in = jnp.sum(attn_in_grad * unit_attn, axis=0)
    input_grad = hidden_grad_in + norm_back(attn_in_grad, unit_attn, root_attn, g_attn_in)
    spread = (2,) * (nseq + nchip + 1)
    count = seq_count * lax.axis_size("dp")
    gains = [grad_g_attn_in, grad_g_attn_out, grad_g_ffn_in, grad_g_ffn_out, grad_g_query, grad_g_key]
    gain_terms = jnp.concatenate([g.reshape(count, -1) for g in gains], axis=1)
    out_term = contract_rows(mixed_b, attn_grad_b)
    qkv_term = contract_rows(attn_input, qkv_grad_b)
    owned_qkv = scatter_ordered(
        qkv_term.reshape(spread + w_qkv.shape), all_up[::-1], jnp.bfloat16
    )
    owned_out = scatter_ordered(
        out_term.reshape(spread + w_out.shape), all_down[::-1], jnp.bfloat16
    )
    owned = scatter_ordered(gain_terms.reshape(spread + (-1,)), all_up[::-1], jnp.float32)
    own_width, own_head = width // count, HEAD_DIM // count
    owned_gains = [owned[i * own_width : (i + 1) * own_width] for i in range(4)]
    owned_heads = [
        owned[4 * own_width + i * own_head : 4 * own_width + (i + 1) * own_head] for i in range(2)
    ]
    return (
        result[None],
        input_grad[None],
        owned_qkv,
        owned_out,
        grad_w_gate,
        grad_w_up,
        grad_w_down,
        owned_gains[0],
        owned_heads[0],
        owned_heads[1],
        owned_gains[1],
        owned_gains[2],
        owned_gains[3],
    )


def solution(mesh):
    return jax.shard_map(
        local,
        mesh=mesh,
        in_specs=(
            P("dp", "seq", None),
            P("dp", "seq", None),
            P("dp", None),
            P(("seq", "dp"), None),
            P(("seq", "dp"), None),
            P(("seq", "dp"), None),
            P(("seq", "dp"), None),
            P(("seq", "dp"), None),
            P(),
            P(),
            P(),
            P(),
            P(),
            P(),
        ),
        out_specs=(
            P("dp", "seq", None),
            P("dp", "seq", None),
            P(("seq", "dp"), None),
            P(("seq", "dp"), None),
            P(("seq", "dp"), None),
            P(("seq", "dp"), None),
            P(("seq", "dp"), None),
            P(("seq", "dp")),
            P(("seq", "dp")),
            P(("seq", "dp")),
            P(("seq", "dp")),
            P(("seq", "dp")),
            P(("seq", "dp")),
        ),
        check_vma=False,
    )
```

```python
import math

import jax
import jax.numpy as jnp
from jax import lax
from jax.sharding import PartitionSpec as P

HEADS = 4
HEAD_DIM = 256
WINDOW = 512


EPSILON = 1e-06
GELU_SLOPE = math.sqrt(2.0 / math.pi)
GELU_CUBIC = 0.044715


def bits_of(count):
    bits = []
    bit = 1
    while bit < count:
        bits.append(bit)
        bit *= 2
    return bits


def swapped(value, axis, bit):
    length = lax.axis_size(axis)
    return lax.ppermute(value, axis, [(i, i ^ bit) for i in range(length)])


def mine_first(value, axis, bit, at):
    return jnp.concatenate([value, swapped(value, axis, bit)], axis=at)


def keep_half(value, axis, bit, at):
    own = lax.slice_in_dim(value, 0, 1, axis=at)
    other = lax.slice_in_dim(value, 1, 2, axis=at).astype(jnp.bfloat16)
    return own.astype(jnp.float32) + swapped(other, axis, bit).astype(jnp.float32)


def scatter_sum(value, stages):
    for axis, bit, at in stages:
        own = lax.slice_in_dim(value, 0, 1, axis=at)
        other = lax.slice_in_dim(value, 1, 2, axis=at)
        value = own + swapped(other, axis, bit)
    return value.reshape(value.shape[len(stages) :])


def gather_xor(value, stages):
    value = value.reshape((1,) * len(stages) + value.shape)
    for axis, bit, at in stages:
        value = mine_first(value, axis, bit, at)
    return value


def scatter_xor(value, stages):
    for axis, bit, at in stages:
        value = keep_half(value, axis, bit, at)
    return value.reshape(value.shape[len(stages) :])


def one_hot_order(origin, count):
    return (jnp.arange(count, dtype=jnp.int32)[:, None] == origin[None, :]).astype(jnp.bfloat16)


def in_order(value, order):
    return lax.dot_general(
        value.astype(jnp.float32),
        order.astype(jnp.float32),
        (((1,), (1,)), ((), ())),
        precision=lax.Precision.HIGHEST,
        preferred_element_type=jnp.float32,
    )


def inv_root(vector):
    return lax.rsqrt(jnp.mean(vector * vector, axis=-1, keepdims=True) + EPSILON)


def norm_back(grad, unit_part, root_part, gain):
    scaled = grad * gain
    return root_part * (scaled - unit_part * jnp.mean(scaled * unit_part, axis=-1, keepdims=True))


def gelu_pair(gate):
    inner = jnp.tanh(GELU_SLOPE * (gate + GELU_CUBIC * gate * gate * gate))
    gelu_value = 0.5 * gate * (1.0 + inner)
    gelu_slope = 0.5 * (1.0 + inner) + 0.5 * gate * (1.0 - inner * inner) * GELU_SLOPE * (
        1.0 + 3.0 * GELU_CUBIC * gate * gate
    )
    return (gelu_value, gelu_slope)


def turn_half(vector):
    half = vector.shape[-1] // 2
    return jnp.concatenate([-vector[..., half:], vector[..., :half]], axis=-1)


def seq_begin(index, starts):
    return jnp.max(jnp.where(starts[None, :] <= index[:, None], starts[None, :], 0), axis=1)


def rope_tables(position, head):
    freq = jnp.exp(-math.log(10000.0) * jnp.arange(head // 2, dtype=jnp.float32) * (2.0 / head))
    angle = position[:, None] * freq[None, :]
    angle = jnp.concatenate([angle, angle], axis=1)
    return (jnp.cos(angle), jnp.sin(angle))


def dot32(left, right):
    return jnp.dot(left, right, preferred_element_type=jnp.float32)


def contract_rows(left, right):
    return lax.dot_general(
        left, right, (((0,), (0,)), ((), ())), preferred_element_type=jnp.float32
    )


def contract_cols(left, right):
    return lax.dot_general(
        left, right, (((1,), (1,)), ((), ())), preferred_element_type=jnp.float32
    )


def ffn_forward_fold(tokens_b, pieces):
    gate_rows, up_rows, down_rows = pieces
    gate_part = contract_cols(tokens_b, gate_rows)
    up_part = contract_cols(tokens_b, up_rows)
    gelu_value, gelu_slope = gelu_pair(gate_part)
    hidden = (gelu_value * up_part).astype(jnp.bfloat16)
    out_total = dot32(hidden, down_rows)
    return (out_total, gate_part, up_part)


def ffn_backward_fold(grad_b, gate_all, up_all, pieces):
    gate_rows, up_rows, down_rows = pieces
    hidden_grad = contract_cols(grad_b, down_rows)
    gelu_value, gelu_slope = gelu_pair(gate_all)
    dgate_b = (hidden_grad * up_all * gelu_slope).astype(jnp.bfloat16)
    dup_b = (hidden_grad * gelu_value).astype(jnp.bfloat16)
    in_total = dot32(dgate_b, gate_rows) + dot32(dup_b, up_rows)
    return (in_total, dgate_b, dup_b)


def ffn_weight_terms(tokens_b, grad_b, gate_all, up_all, dgate_all, dup_all):
    gelu_value, gelu_slope = gelu_pair(gate_all)
    hidden = (gelu_value * up_all).astype(jnp.bfloat16)
    return (
        contract_rows(dgate_all, tokens_b),
        contract_rows(dup_all, tokens_b),
        contract_rows(hidden, grad_b),
    )


def local(
    stream,
    stream_grad,
    lengths,
    w_qkv,
    w_out,
    w_gate,
    w_up,
    w_down,
    g_attn_in,
    g_query,
    g_key,
    g_attn_out,
    g_ffn_in,
    g_ffn_out,
):
    rows_in = stream[0]
    rows_grad = stream_grad[0]
    lens = lengths[0]
    rows = rows_in.shape[0]
    width = rows_in.shape[1]
    qwidth = HEADS * HEAD_DIM
    seq_count = lax.axis_size("seq")
    chip_bits = [2 * bit for bit in bits_of(lax.axis_size("dp") // 2)]
    seq_bits = bits_of(seq_count)
    nseq, nchip = len(seq_bits), len(chip_bits)
    seq_stages = [("seq", bit, nseq - 1 - k) for k, bit in enumerate(seq_bits)][::-1]
    chip_stages = [("dp", bit, nseq + nchip - 1 - k) for k, bit in enumerate(chip_bits)]
    core_stage = [("dp", 1, nseq + nchip)]
    all_up = seq_stages + chip_stages + core_stage
    all_down = seq_stages + chip_stages[::-1] + core_stage
    dp_count = lax.axis_size("dp")
    chips = dp_count // 2
    planes = [[2 * chip + core for chip in range(chips)] for core in range(2)]
    kv_stages = seq_stages
    seq_stages_only = seq_stages
    token_stages = seq_stages + [("dp", 1, nseq)]
    keys = seq_count * rows
    scale = 1.0 / math.sqrt(HEAD_DIM)
    block_id = lax.axis_index("seq")
    dp_id = lax.axis_index("dp")
    seq_off = jnp.arange(seq_count, dtype=jnp.int32)
    chip_off = jnp.arange(chips, dtype=jnp.int32)
    core_off = jnp.arange(2, dtype=jnp.int32)
    qkv_own = w_qkv.shape[0]
    qkv_pad = (qkv_own + 7) // 8 * 8
    out_own = w_out.shape[0]
    ffn_own = w_gate.shape[0]
    half = w_qkv.shape[1] // 2
    qkv_dev = (
        (block_id ^ seq_off)[:, None, None] * dp_count
        + ((dp_id // 2) ^ chip_off)[None, :, None] * 2
        + ((dp_id % 2) ^ core_off)[None, None, :]
    ).reshape(-1, 1)
    lane = jnp.arange(qkv_pad, dtype=jnp.int32)[None, :]
    qkv_origin = jnp.where(lane < qkv_own, qkv_dev * qkv_own + lane, -1).reshape(-1)
    out_dev = (
        (block_id ^ seq_off)[None, None, :] * dp_count
        + chip_off[None, :, None] * 2
        + ((dp_id % 2) ^ core_off)[:, None, None]
    ).reshape(-1, 1)
    out_origin = (out_dev * out_own + jnp.arange(out_own, dtype=jnp.int32)[None, :]).reshape(-1)
    qkv_order = one_hot_order(qkv_origin, width)
    out_order = one_hot_order(out_origin, qwidth)
    w_qkv_pad = jnp.pad(w_qkv, ((0, qkv_pad - qkv_own), (0, 0)))
    qkv_full = jnp.concatenate(
        [
            gather_xor(w_qkv_pad[:, :half], all_up),
            gather_xor(w_qkv_pad[:, half:], all_down),
        ],
        axis=-1,
    ).reshape(-1, 2 * half)
    out_column = gather_xor(w_out, seq_stages_only).reshape(-1, width)
    plane_rows = lax.all_gather(
        jnp.concatenate([w_gate, w_up, w_down, out_column], axis=0),
        "dp",
        axis_index_groups=planes,
        axis=0,
    )
    gate_full, up_full, down_full = (
        plane_rows[:, i * ffn_own : (i + 1) * ffn_own].reshape(-1, width) for i in range(3)
    )
    out_full = mine_first(plane_rows[None, :, 3 * ffn_own :], "dp", 1, 0).reshape(-1, width)
    starts = jnp.cumsum(lens) - lens
    own_index = block_id * rows + jnp.arange(rows, dtype=jnp.int32)
    key_index = (
        (block_id ^ jnp.arange(seq_count, dtype=jnp.int32))[:, None] * rows
        + jnp.arange(rows, dtype=jnp.int32)[None, :]
    ).reshape(keys)
    own_begin = seq_begin(own_index, starts)
    key_begin = seq_begin(key_index, starts)
    mask = (
        (key_begin[None, :] == own_begin[:, None])
        & (key_index[None, :] <= own_index[:, None])
        & (own_index[:, None] - key_index[None, :] < WINDOW)
    )
    full_mask = mask[:, None, :]
    cos_t, sin_t = rope_tables((own_index - own_begin).astype(jnp.float32), HEAD_DIM)
    root_attn = inv_root(rows_in)
    unit_attn = rows_in * root_attn
    attn_input = (unit_attn * g_attn_in).astype(jnp.bfloat16)
    attn_slots = dot32(attn_input, qkv_order).astype(jnp.bfloat16)
    projected = dot32(attn_slots, qkv_full)
    query = projected[:, :qwidth].reshape(rows, HEADS, HEAD_DIM)
    key_raw = projected[:, qwidth : qwidth + HEAD_DIM]
    value_raw = projected[:, qwidth + HEAD_DIM :]
    root_query = inv_root(query)
    unit_query = query * root_query
    query_norm = unit_query * g_query
    root_key = inv_root(key_raw)
    unit_key = key_raw * root_key
    key_norm = unit_key * g_key
    query_rot = query_norm * cos_t[:, None, :] + turn_half(query_norm) * sin_t[:, None, :]
    key_rot = key_norm * cos_t + turn_half(key_norm) * sin_t
    query_b = query_rot.astype(jnp.bfloat16)
    kv_own = jnp.concatenate([key_rot.astype(jnp.bfloat16), value_raw.astype(jnp.bfloat16)], axis=1)
    kv_all = gather_xor(kv_own, kv_stages).reshape(keys, 2 * HEAD_DIM)
    keys_b = kv_all[:, :HEAD_DIM]
    values_b = kv_all[:, HEAD_DIM:]
    scores = jnp.einsum("rhd,kd->rhk", query_b, keys_b, preferred_element_type=jnp.float32) * scale
    logsum = jnp.log(jnp.sum(jnp.where(full_mask, jnp.exp(scores), 0.0), axis=-1))
    probs = jnp.where(full_mask, jnp.exp(scores - logsum[..., None]), 0.0)
    probs_b = probs.astype(jnp.bfloat16)
    mixed = jnp.einsum("rhk,kd->rhd", probs_b, values_b, preferred_element_type=jnp.float32)
    mixed_b = mixed.reshape(rows, qwidth).astype(jnp.bfloat16)
    mixed_slots = dot32(mixed_b, out_order).astype(jnp.bfloat16)
    attn_out = dot32(mixed_slots, out_full)
    root_post = inv_root(attn_out)
    unit_post = attn_out * root_post
    hidden_in = rows_in + unit_post * g_attn_out
    root_ffn = inv_root(hidden_in)
    unit_ffn = hidden_in * root_ffn
    ffn_input = (unit_ffn * g_ffn_in).astype(jnp.bfloat16)
    slots = (2,) * len(token_stages)
    tokens_b = gather_xor(ffn_input, token_stages).reshape(-1, width)
    out_part, gate_all, up_all = ffn_forward_fold(tokens_b, (gate_full, up_full, down_full))
    ffn_out = scatter_xor(out_part.reshape(slots + (rows, width)), token_stages[::-1])
    root_out = inv_root(ffn_out)
    unit_out = ffn_out * root_out
    result = hidden_in + unit_out * g_ffn_out
    grad_g_ffn_out = jnp.sum(rows_grad * unit_out, axis=0)
    ffn_grad_b = norm_back(rows_grad, unit_out, root_out, g_ffn_out).astype(jnp.bfloat16)
    grads_b = gather_xor(ffn_grad_b, token_stages).reshape(-1, width)
    in_part, dgate_all, dup_all = ffn_backward_fold(
        grads_b, gate_all, up_all, (gate_full, up_full, down_full)
    )
    ffn_in_grad = scatter_xor(in_part.reshape(slots + (rows, width)), token_stages[::-1])
    terms = ffn_weight_terms(tokens_b, grads_b, gate_all, up_all, dgate_all, dup_all)
    ffn_terms = lax.psum_scatter(
        jnp.concatenate(
            [term.astype(jnp.bfloat16).reshape(chips, ffn_own, width) for term in terms], axis=1
        ),
        "dp",
        axis_index_groups=planes,
        scatter_dimension=0,
    ).astype(jnp.float32)
    ffn_terms = ffn_terms.reshape(3, ffn_own, width)
    grad_w_gate, grad_w_up, grad_w_down = ffn_terms[0], ffn_terms[1], ffn_terms[2]
    grad_g_ffn_in = jnp.sum(ffn_in_grad * unit_ffn, axis=0)
    hidden_grad_in = rows_grad + norm_back(ffn_in_grad, unit_ffn, root_ffn, g_ffn_in)
    grad_g_attn_out = jnp.sum(hidden_grad_in * unit_post, axis=0)
    attn_grad_b = norm_back(hidden_grad_in, unit_post, root_post, g_attn_out).astype(jnp.bfloat16)
    mixed_grad_slots = contract_cols(attn_grad_b, out_full).astype(jnp.bfloat16)
    mixed_grad_b = contract_cols(mixed_grad_slots, out_order).astype(jnp.bfloat16)
    out_term = contract_rows(mixed_slots, attn_grad_b).reshape(2, chips, -1, width)
    out_plane = lax.psum_scatter(
        keep_half(out_term, "dp", 1, 0)[0].astype(jnp.bfloat16),
        "dp",
        axis_index_groups=planes,
        scatter_dimension=0,
    ).astype(jnp.float32)
    owned_out = scatter_xor(
        out_plane.reshape((2,) * nseq + w_out.shape), seq_stages[::-1]
    )
    mixed_grad3 = mixed_grad_b.reshape(rows, HEADS, HEAD_DIM)
    delta = jnp.sum(
        mixed_grad3.astype(jnp.float32)
        * mixed_b.reshape(rows, HEADS, HEAD_DIM).astype(jnp.float32),
        axis=-1,
    )
    scores_again = (
        jnp.einsum("rhd,kd->rhk", query_b, keys_b, preferred_element_type=jnp.float32) * scale
    )
    probs_again = jnp.where(full_mask, jnp.exp(scores_again - logsum[..., None]), 0.0)
    probs_again_b = probs_again.astype(jnp.bfloat16)
    value_grad_all = jnp.einsum(
        "rhk,rhd->kd", probs_again_b, mixed_grad3, preferred_element_type=jnp.float32
    )
    prob_grad = jnp.einsum("rhd,kd->rhk", mixed_grad3, values_b, preferred_element_type=jnp.float32)
    score_grad_b = (probs_again * (prob_grad - delta[..., None])).astype(jnp.bfloat16)
    query_rot_grad = (
        jnp.einsum("rhk,kd->rhd", score_grad_b, keys_b, preferred_element_type=jnp.float32) * scale
    )
    key_grad_all = (
        jnp.einsum("rhk,rhd->kd", score_grad_b, query_b, preferred_element_type=jnp.float32) * scale
    )
    kv_grad_all = jnp.concatenate([key_grad_all, value_grad_all], axis=1)
    kv_grad = scatter_xor(
        kv_grad_all.reshape((2,) * nseq + (rows, 2 * HEAD_DIM)), kv_stages[::-1]
    )
    key_rot_grad = kv_grad[:, :HEAD_DIM]
    value_grad = kv_grad[:, HEAD_DIM:]
    query_norm_grad = query_rot_grad * cos_t[:, None, :] - turn_half(
        query_rot_grad * sin_t[:, None, :]
    )
    key_norm_grad = key_rot_grad * cos_t - turn_half(key_rot_grad * sin_t)
    grad_g_query = jnp.sum(query_norm_grad * unit_query, axis=(0, 1))
    grad_g_key = jnp.sum(key_norm_grad * unit_key, axis=0)
    query_grad = norm_back(query_norm_grad, unit_query, root_query, g_query)
    key_grad = norm_back(key_norm_grad, unit_key, root_key, g_key)
    qkv_grad_b = jnp.concatenate(
        [query_grad.reshape(rows, qwidth), key_grad, value_grad], axis=1
    ).astype(jnp.bfloat16)
    attn_in_grad = in_order(contract_cols(qkv_grad_b, qkv_full), qkv_order)
    grad_g_attn_in = jnp.sum(attn_in_grad * unit_attn, axis=0)
    input_grad = hidden_grad_in + norm_back(attn_in_grad, unit_attn, root_attn, g_attn_in)
    spread = (2,) * (nseq + nchip + 1)
    count = seq_count * lax.axis_size("dp")
    gains = [grad_g_attn_in, grad_g_attn_out, grad_g_ffn_in, grad_g_ffn_out, grad_g_query, grad_g_key]
    gain_terms = jnp.concatenate([g.reshape(count, -1) for g in gains], axis=1)
    qkv_term = contract_rows(attn_slots, qkv_grad_b).reshape(spread + (qkv_pad, 2 * half))
    owned_qkv = jnp.concatenate(
        [
            scatter_xor(qkv_term[..., :half], all_up[::-1]),
            scatter_xor(qkv_term[..., half:], all_down[::-1]),
        ],
        axis=-1,
    )[:qkv_own]
    gain_slots = jnp.take(gain_terms, qkv_dev.reshape(-1), axis=0)
    owned = scatter_sum(gain_slots.reshape(spread + (-1,)), all_up[::-1])
    own_width, own_head = width // count, HEAD_DIM // count
    owned_gains = [owned[i * own_width : (i + 1) * own_width] for i in range(4)]
    owned_heads = [
        owned[4 * own_width + i * own_head : 4 * own_width + (i + 1) * own_head] for i in range(2)
    ]
    return (
        result[None],
        input_grad[None],
        owned_qkv,
        owned_out,
        grad_w_gate,
        grad_w_up,
        grad_w_down,
        owned_gains[0],
        owned_heads[0],
        owned_heads[1],
        owned_gains[1],
        owned_gains[2],
        owned_gains[3],
    )


def solution(mesh):
    return jax.shard_map(
        local,
        mesh=mesh,
        in_specs=(
            P("dp", "seq", None),
            P("dp", "seq", None),
            P("dp", None),
            P(("seq", "dp"), None),
            P(("seq", "dp"), None),
            P(("seq", "dp"), None),
            P(("seq", "dp"), None),
            P(("seq", "dp"), None),
            P(),
            P(),
            P(),
            P(),
            P(),
            P(),
        ),
        out_specs=(
            P("dp", "seq", None),
            P("dp", "seq", None),
            P(("seq", "dp"), None),
            P(("seq", "dp"), None),
            P(("seq", "dp"), None),
            P(("seq", "dp"), None),
            P(("seq", "dp"), None),
            P(("seq", "dp")),
            P(("seq", "dp")),
            P(("seq", "dp")),
            P(("seq", "dp")),
            P(("seq", "dp")),
            P(("seq", "dp")),
        ),
        check_vma=False,
    )
```

```python
import math

import jax
import jax.numpy as jnp
from jax import lax
from jax.sharding import PartitionSpec as P

HEADS = 4
HEAD_DIM = 256
WINDOW = 512


EPSILON = 1e-06
GELU_SLOPE = math.sqrt(2.0 / math.pi)
GELU_CUBIC = 0.044715


def bits_of(count):
    bits = []
    bit = 1
    while bit < count:
        bits.append(bit)
        bit *= 2
    return bits


def swapped(value, axis, bit):
    length = lax.axis_size(axis)
    return lax.ppermute(value, axis, [(i, i ^ bit) for i in range(length)])


def mine_first(value, axis, bit, at):
    return jnp.concatenate([value, swapped(value, axis, bit)], axis=at)


def keep_half(value, axis, bit, at):
    own = lax.slice_in_dim(value, 0, 1, axis=at)
    other = lax.slice_in_dim(value, 1, 2, axis=at).astype(jnp.bfloat16)
    return own.astype(jnp.float32) + swapped(other, axis, bit).astype(jnp.float32)


def gather_xor(value, stages):
    value = value.reshape((1,) * len(stages) + value.shape)
    for axis, bit, at in stages:
        value = mine_first(value, axis, bit, at)
    return value


def scatter_xor(value, stages):
    for axis, bit, at in stages:
        value = keep_half(value, axis, bit, at)
    return value.reshape(value.shape[len(stages) :])


def one_hot_order(origin, count):
    return (jnp.arange(count, dtype=jnp.int32)[:, None] == origin[None, :]).astype(jnp.bfloat16)


def in_order(value, order):
    return lax.dot_general(
        value.astype(jnp.float32),
        order.astype(jnp.float32),
        (((1,), (1,)), ((), ())),
        precision=lax.Precision.HIGHEST,
        preferred_element_type=jnp.float32,
    )


def inv_root(vector):
    return lax.rsqrt(jnp.mean(vector * vector, axis=-1, keepdims=True) + EPSILON)


def norm_back(grad, unit_part, root_part, gain):
    scaled = grad * gain
    return root_part * (scaled - unit_part * jnp.mean(scaled * unit_part, axis=-1, keepdims=True))


def gelu_pair(gate):
    inner = jnp.tanh(GELU_SLOPE * (gate + GELU_CUBIC * gate * gate * gate))
    gelu_value = 0.5 * gate * (1.0 + inner)
    gelu_slope = 0.5 * (1.0 + inner) + 0.5 * gate * (1.0 - inner * inner) * GELU_SLOPE * (
        1.0 + 3.0 * GELU_CUBIC * gate * gate
    )
    return (gelu_value, gelu_slope)


def turn_half(vector):
    half = vector.shape[-1] // 2
    return jnp.concatenate([-vector[..., half:], vector[..., :half]], axis=-1)


def seq_begin(index, starts):
    return jnp.max(jnp.where(starts[None, :] <= index[:, None], starts[None, :], 0), axis=1)


def rope_tables(position, head):
    freq = jnp.exp(-math.log(10000.0) * jnp.arange(head // 2, dtype=jnp.float32) * (2.0 / head))
    angle = position[:, None] * freq[None, :]
    angle = jnp.concatenate([angle, angle], axis=1)
    return (jnp.cos(angle), jnp.sin(angle))


def dot32(left, right):
    return jnp.dot(left, right, preferred_element_type=jnp.float32)


def contract_rows(left, right):
    return lax.dot_general(
        left, right, (((0,), (0,)), ((), ())), preferred_element_type=jnp.float32
    )


def contract_cols(left, right):
    return lax.dot_general(
        left, right, (((1,), (1,)), ((), ())), preferred_element_type=jnp.float32
    )


def ffn_forward_fold(tokens_b, pieces):
    gate_rows, up_rows, down_rows = pieces
    gate_part = contract_cols(tokens_b, gate_rows)
    up_part = contract_cols(tokens_b, up_rows)
    gelu_value, gelu_slope = gelu_pair(gate_part)
    hidden = (gelu_value * up_part).astype(jnp.bfloat16)
    out_total = dot32(hidden, down_rows)
    return (out_total, gate_part, up_part)


def ffn_backward_fold(grad_b, gate_all, up_all, pieces):
    gate_rows, up_rows, down_rows = pieces
    hidden_grad = contract_cols(grad_b, down_rows)
    gelu_value, gelu_slope = gelu_pair(gate_all)
    dgate_b = (hidden_grad * up_all * gelu_slope).astype(jnp.bfloat16)
    dup_b = (hidden_grad * gelu_value).astype(jnp.bfloat16)
    in_total = dot32(dgate_b, gate_rows) + dot32(dup_b, up_rows)
    return (in_total, dgate_b, dup_b)


def ffn_weight_terms(tokens_b, grad_b, gate_all, up_all, dgate_all, dup_all):
    gelu_value, gelu_slope = gelu_pair(gate_all)
    hidden = (gelu_value * up_all).astype(jnp.bfloat16)
    return (
        contract_rows(dgate_all, tokens_b),
        contract_rows(dup_all, tokens_b),
        contract_rows(hidden, grad_b),
    )


def local(
    stream,
    stream_grad,
    lengths,
    w_qkv,
    w_out,
    w_gate,
    w_up,
    w_down,
    g_attn_in,
    g_query,
    g_key,
    g_attn_out,
    g_ffn_in,
    g_ffn_out,
):
    rows_in = stream[0]
    rows_grad = stream_grad[0]
    lens = lengths[0]
    rows = rows_in.shape[0]
    width = rows_in.shape[1]
    qwidth = HEADS * HEAD_DIM
    seq_count = lax.axis_size("seq")
    chip_bits = [2 * bit for bit in bits_of(lax.axis_size("dp") // 2)]
    seq_bits = bits_of(seq_count)
    nseq, nchip = len(seq_bits), len(chip_bits)
    seq_stages = [("seq", bit, nseq - 1 - k) for k, bit in enumerate(seq_bits)][::-1]
    chip_stages = [("dp", bit, nseq + nchip - 1 - k) for k, bit in enumerate(chip_bits)]
    core_stage = [("dp", 1, nseq + nchip)]
    all_up = seq_stages + chip_stages + core_stage
    all_down = seq_stages + chip_stages[::-1] + core_stage
    dp_count = lax.axis_size("dp")
    chips = dp_count // 2
    plane_up = [("dp", bit, nchip - 1 - k) for k, bit in enumerate(chip_bits)]
    plane_down = plane_up[::-1]
    cut = (width // 256) * 128 + (128 if width % 256 else 0)
    kv_stages = seq_stages
    keys = seq_count * rows
    scale = 1.0 / math.sqrt(HEAD_DIM)
    block_id = lax.axis_index("seq")
    dp_id = lax.axis_index("dp")
    seq_off = jnp.arange(seq_count, dtype=jnp.int32)
    chip_off = jnp.arange(chips, dtype=jnp.int32)
    core_off = jnp.arange(2, dtype=jnp.int32)
    qkv_own = w_qkv.shape[0]
    qkv_pad = (qkv_own + 8) // 8 * 8
    out_own = w_out.shape[0]
    ffn_own = w_gate.shape[0]
    half = w_qkv.shape[1] // 2
    qkv_dev = (
        (block_id ^ seq_off)[:, None, None] * dp_count
        + ((dp_id // 2) ^ chip_off)[None, :, None] * 2
        + ((dp_id % 2) ^ core_off)[None, None, :]
    ).reshape(-1, 1)
    lane = jnp.arange(qkv_pad, dtype=jnp.int32)[None, :]
    qkv_origin = jnp.where(lane < qkv_own, qkv_dev * qkv_own + lane, -1).reshape(-1)
    out_dev = (
        seq_off[None, :, None] * dp_count
        + ((dp_id // 2) ^ chip_off)[None, None, :] * 2
        + ((dp_id % 2) ^ core_off)[:, None, None]
    ).reshape(-1, 1)
    out_origin = (out_dev * out_own + jnp.arange(out_own, dtype=jnp.int32)[None, :]).reshape(-1)
    qkv_order = one_hot_order(qkv_origin, width)
    out_order = one_hot_order(out_origin, qwidth)
    w_qkv_pad = jnp.pad(w_qkv, ((0, qkv_pad - qkv_own), (0, 0)))
    qkv_full = jnp.concatenate(
        [
            gather_xor(w_qkv_pad[:, :half], all_up),
            gather_xor(w_qkv_pad[:, half:], all_down),
        ],
        axis=-1,
    ).reshape(-1, 2 * half)
    out_column = gather_xor(w_out, plane_up).reshape(-1, width)
    line_rows = lax.all_gather(
        jnp.concatenate([w_gate, w_up, w_down, out_column], axis=0),
        "seq",
        axis=0,
    )
    gate_full, up_full, down_full = (
        line_rows[:, i * ffn_own : (i + 1) * ffn_own].reshape(-1, width) for i in range(3)
    )
    out_full = mine_first(line_rows[None, :, 3 * ffn_own :], "dp", 1, 0).reshape(-1, width)
    starts = jnp.cumsum(lens) - lens
    own_index = block_id * rows + jnp.arange(rows, dtype=jnp.int32)
    key_index = (
        (block_id ^ jnp.arange(seq_count, dtype=jnp.int32))[:, None] * rows
        + jnp.arange(rows, dtype=jnp.int32)[None, :]
    ).reshape(keys)
    own_begin = seq_begin(own_index, starts)
    key_begin = seq_begin(key_index, starts)
    mask = (
        (key_begin[None, :] == own_begin[:, None])
        & (key_index[None, :] <= own_index[:, None])
        & (own_index[:, None] - key_index[None, :] < WINDOW)
    )
    full_mask = mask[:, None, :]
    cos_t, sin_t = rope_tables((own_index - own_begin).astype(jnp.float32), HEAD_DIM)
    root_attn = inv_root(rows_in)
    unit_attn = rows_in * root_attn
    attn_input = (unit_attn * g_attn_in).astype(jnp.bfloat16)
    attn_slots = dot32(attn_input, qkv_order).astype(jnp.bfloat16)
    projected = dot32(attn_slots, qkv_full)
    query = projected[:, :qwidth].reshape(rows, HEADS, HEAD_DIM)
    key_raw = projected[:, qwidth : qwidth + HEAD_DIM]
    value_raw = projected[:, qwidth + HEAD_DIM :]
    root_query = inv_root(query)
    unit_query = query * root_query
    query_norm = unit_query * g_query
    root_key = inv_root(key_raw)
    unit_key = key_raw * root_key
    key_norm = unit_key * g_key
    query_rot = query_norm * cos_t[:, None, :] + turn_half(query_norm) * sin_t[:, None, :]
    key_rot = key_norm * cos_t + turn_half(key_norm) * sin_t
    query_b = query_rot.astype(jnp.bfloat16)
    kv_own = jnp.concatenate([key_rot.astype(jnp.bfloat16), value_raw.astype(jnp.bfloat16)], axis=1)
    kv_all = gather_xor(kv_own, kv_stages).reshape(keys, 2 * HEAD_DIM)
    keys_b = kv_all[:, :HEAD_DIM]
    values_b = kv_all[:, HEAD_DIM:]
    scores = jnp.einsum("rhd,kd->rhk", query_b, keys_b, preferred_element_type=jnp.float32) * scale
    logsum = jnp.log(jnp.sum(jnp.where(full_mask, jnp.exp(scores), 0.0), axis=-1))
    probs = jnp.where(full_mask, jnp.exp(scores - logsum[..., None]), 0.0)
    probs_b = probs.astype(jnp.bfloat16)
    mixed = jnp.einsum("rhk,kd->rhd", probs_b, values_b, preferred_element_type=jnp.float32)
    mixed_b = mixed.reshape(rows, qwidth).astype(jnp.bfloat16)
    mixed_slots = dot32(mixed_b, out_order).astype(jnp.bfloat16)
    attn_out = dot32(mixed_slots, out_full)
    root_post = inv_root(attn_out)
    unit_post = attn_out * root_post
    hidden_in = rows_in + unit_post * g_attn_out
    root_ffn = inv_root(hidden_in)
    unit_ffn = hidden_in * root_ffn
    ffn_input = (unit_ffn * g_ffn_in).astype(jnp.bfloat16)

    def gather_tokens(value):
        both = jnp.concatenate(
            [gather_xor(value[:, :cut], plane_up), gather_xor(value[:, cut:], plane_down)], axis=-1
        )
        return mine_first(both[None], "dp", 1, 0).reshape(-1, width)

    def scatter_tokens(value):
        value = keep_half(value.reshape((2,) * (1 + nchip) + (rows, width)), "dp", 1, 0)[0]
        return jnp.concatenate(
            [
                scatter_xor(value[..., :cut], plane_down),
                scatter_xor(value[..., cut:], plane_up),
            ],
            axis=-1,
        )

    tokens_b = gather_tokens(ffn_input)
    out_part, gate_all, up_all = ffn_forward_fold(tokens_b, (gate_full, up_full, down_full))
    ffn_out = scatter_tokens(out_part)
    root_out = inv_root(ffn_out)
    unit_out = ffn_out * root_out
    result = hidden_in + unit_out * g_ffn_out
    grad_g_ffn_out = jnp.sum(rows_grad * unit_out, axis=0)
    ffn_grad_b = norm_back(rows_grad, unit_out, root_out, g_ffn_out).astype(jnp.bfloat16)
    grads_b = gather_tokens(ffn_grad_b)
    in_part, dgate_all, dup_all = ffn_backward_fold(
        grads_b, gate_all, up_all, (gate_full, up_full, down_full)
    )
    ffn_in_grad = scatter_tokens(in_part)
    terms = ffn_weight_terms(tokens_b, grads_b, gate_all, up_all, dgate_all, dup_all)
    ffn_in_grad, term_rows = lax.optimization_barrier(
        (
            ffn_in_grad,
            jnp.concatenate(
                [term.astype(jnp.bfloat16).reshape(seq_count, ffn_own, width) for term in terms],
                axis=1,
            ),
        )
    )
    ffn_terms = lax.psum_scatter(term_rows, "seq", scatter_dimension=0).astype(jnp.float32)
    ffn_terms = ffn_terms.reshape(3, ffn_own, width)
    grad_w_gate, grad_w_up, grad_w_down = ffn_terms[0], ffn_terms[1], ffn_terms[2]
    grad_g_ffn_in = jnp.sum(ffn_in_grad * unit_ffn, axis=0)
    hidden_grad_in = rows_grad + norm_back(ffn_in_grad, unit_ffn, root_ffn, g_ffn_in)
    grad_g_attn_out = jnp.sum(hidden_grad_in * unit_post, axis=0)
    attn_grad_b = norm_back(hidden_grad_in, unit_post, root_post, g_attn_out).astype(jnp.bfloat16)
    mixed_grad_slots = contract_cols(attn_grad_b, out_full).astype(jnp.bfloat16)
    mixed_grad_b = contract_cols(mixed_grad_slots, out_order).astype(jnp.bfloat16)
    out_term = contract_rows(mixed_slots, attn_grad_b).reshape(2, seq_count, -1, width)
    out_line = lax.psum_scatter(
        keep_half(out_term, "dp", 1, 0)[0].astype(jnp.bfloat16),
        "seq",
        scatter_dimension=0,
    ).astype(jnp.float32)
    owned_out = scatter_xor(
        out_line.reshape((2,) * nchip + w_out.shape), plane_down
    )
    mixed_grad3 = mixed_grad_b.reshape(rows, HEADS, HEAD_DIM)
    delta = jnp.sum(
        mixed_grad3.astype(jnp.float32)
        * mixed_b.reshape(rows, HEADS, HEAD_DIM).astype(jnp.float32),
        axis=-1,
    )
    scores_again = (
        jnp.einsum("rhd,kd->rhk", query_b, keys_b, preferred_element_type=jnp.float32) * scale
    )
    probs_again = jnp.where(full_mask, jnp.exp(scores_again - logsum[..., None]), 0.0)
    probs_again_b = probs_again.astype(jnp.bfloat16)
    value_grad_all = jnp.einsum(
        "rhk,rhd->kd", probs_again_b, mixed_grad3, preferred_element_type=jnp.float32
    )
    prob_grad = jnp.einsum("rhd,kd->rhk", mixed_grad3, values_b, preferred_element_type=jnp.float32)
    score_grad_b = (probs_again * (prob_grad - delta[..., None])).astype(jnp.bfloat16)
    query_rot_grad = (
        jnp.einsum("rhk,kd->rhd", score_grad_b, keys_b, preferred_element_type=jnp.float32) * scale
    )
    key_grad_all = (
        jnp.einsum("rhk,rhd->kd", score_grad_b, query_b, preferred_element_type=jnp.float32) * scale
    )
    kv_grad_all = jnp.concatenate([key_grad_all, value_grad_all], axis=1)
    kv_grad = scatter_xor(
        kv_grad_all.reshape((2,) * nseq + (rows, 2 * HEAD_DIM)), kv_stages[::-1]
    )
    key_rot_grad = kv_grad[:, :HEAD_DIM]
    value_grad = kv_grad[:, HEAD_DIM:]
    query_norm_grad = query_rot_grad * cos_t[:, None, :] - turn_half(
        query_rot_grad * sin_t[:, None, :]
    )
    key_norm_grad = key_rot_grad * cos_t - turn_half(key_rot_grad * sin_t)
    grad_g_query = jnp.sum(query_norm_grad * unit_query, axis=(0, 1))
    grad_g_key = jnp.sum(key_norm_grad * unit_key, axis=0)
    query_grad = norm_back(query_norm_grad, unit_query, root_query, g_query)
    key_grad = norm_back(key_norm_grad, unit_key, root_key, g_key)
    qkv_grad_b = jnp.concatenate(
        [query_grad.reshape(rows, qwidth), key_grad, value_grad], axis=1
    ).astype(jnp.bfloat16)
    attn_in_grad = in_order(contract_cols(qkv_grad_b, qkv_full), qkv_order)
    grad_g_attn_in = jnp.sum(attn_in_grad * unit_attn, axis=0)
    input_grad = hidden_grad_in + norm_back(attn_in_grad, unit_attn, root_attn, g_attn_in)
    spread = (2,) * (nseq + nchip + 1)
    count = seq_count * lax.axis_size("dp")
    gains = [grad_g_attn_in, grad_g_attn_out, grad_g_ffn_in, grad_g_ffn_out, grad_g_query, grad_g_key]
    gain_terms = jnp.concatenate([g.reshape(count, -1) for g in gains], axis=1)
    qkv_term = contract_rows(attn_slots, qkv_grad_b).reshape(spread + (qkv_pad, 2 * half))
    gain_slots = jnp.take(gain_terms, qkv_dev.reshape(-1), axis=0)
    left_term = qkv_term[..., :half].at[..., qkv_own, : gain_slots.shape[1]].set(
        gain_slots.reshape(spread + (-1,))
    )
    left_owned = scatter_xor(left_term, all_up[::-1])
    right_owned = scatter_xor(qkv_term[..., half:], all_down[::-1])
    owned_qkv = jnp.concatenate([left_owned, right_owned], axis=-1)[:qkv_own]
    owned = left_owned[qkv_own]
    own_width, own_head = width // count, HEAD_DIM // count
    owned_gains = [owned[i * own_width : (i + 1) * own_width] for i in range(4)]
    owned_heads = [
        owned[4 * own_width + i * own_head : 4 * own_width + (i + 1) * own_head] for i in range(2)
    ]
    return (
        result[None],
        input_grad[None],
        owned_qkv,
        owned_out,
        grad_w_gate,
        grad_w_up,
        grad_w_down,
        owned_gains[0],
        owned_heads[0],
        owned_heads[1],
        owned_gains[1],
        owned_gains[2],
        owned_gains[3],
    )


def solution(mesh):
    return jax.shard_map(
        local,
        mesh=mesh,
        in_specs=(
            P("dp", "seq", None),
            P("dp", "seq", None),
            P("dp", None),
            P(("seq", "dp"), None),
            P(("seq", "dp"), None),
            P(("seq", "dp"), None),
            P(("seq", "dp"), None),
            P(("seq", "dp"), None),
            P(),
            P(),
            P(),
            P(),
            P(),
            P(),
        ),
        out_specs=(
            P("dp", "seq", None),
            P("dp", "seq", None),
            P(("seq", "dp"), None),
            P(("seq", "dp"), None),
            P(("seq", "dp"), None),
            P(("seq", "dp"), None),
            P(("seq", "dp"), None),
            P(("seq", "dp")),
            P(("seq", "dp")),
            P(("seq", "dp")),
            P(("seq", "dp")),
            P(("seq", "dp")),
            P(("seq", "dp")),
        ),
        check_vma=False,
    )
```

```python
import math

import jax
import jax.numpy as jnp
from jax import lax
from jax.sharding import PartitionSpec as P

HEADS = 4
HEAD_DIM = 256
WINDOW = 512


EPSILON = 1e-06
GELU_SLOPE = math.sqrt(2.0 / math.pi)
GELU_CUBIC = 0.044715


def bits_of(count):
    bits = []
    bit = 1
    while bit < count:
        bits.append(bit)
        bit *= 2
    return bits


def swapped(value, axis, bit):
    length = lax.axis_size(axis)
    return lax.ppermute(value, axis, [(i, i ^ bit) for i in range(length)])


def mine_first(value, axis, bit, at):
    return jnp.concatenate([value, swapped(value, axis, bit)], axis=at)


def keep_half(value, axis, bit, at):
    own = lax.slice_in_dim(value, 0, 1, axis=at)
    other = lax.slice_in_dim(value, 1, 2, axis=at).astype(jnp.bfloat16)
    return own.astype(jnp.float32) + swapped(other, axis, bit).astype(jnp.float32)


def gather_xor(value, stages):
    value = value.reshape((1,) * len(stages) + value.shape)
    for axis, bit, at in stages:
        value = mine_first(value, axis, bit, at)
    return value


def scatter_xor(value, stages):
    for axis, bit, at in stages:
        value = keep_half(value, axis, bit, at)
    return value.reshape(value.shape[len(stages) :])


def one_hot_order(origin, count):
    return (jnp.arange(count, dtype=jnp.int32)[:, None] == origin[None, :]).astype(jnp.bfloat16)


def in_order(value, order):
    return lax.dot_general(
        value.astype(jnp.float32),
        order.astype(jnp.float32),
        (((1,), (1,)), ((), ())),
        precision=lax.Precision.HIGHEST,
        preferred_element_type=jnp.float32,
    )


def inv_root(vector):
    return lax.rsqrt(jnp.mean(vector * vector, axis=-1, keepdims=True) + EPSILON)


def norm_back(grad, unit_part, root_part, gain):
    scaled = grad * gain
    return root_part * (scaled - unit_part * jnp.mean(scaled * unit_part, axis=-1, keepdims=True))


def gelu_pair(gate):
    inner = jnp.tanh(GELU_SLOPE * (gate + GELU_CUBIC * gate * gate * gate))
    gelu_value = 0.5 * gate * (1.0 + inner)
    gelu_slope = 0.5 * (1.0 + inner) + 0.5 * gate * (1.0 - inner * inner) * GELU_SLOPE * (
        1.0 + 3.0 * GELU_CUBIC * gate * gate
    )
    return (gelu_value, gelu_slope)


def turn_half(vector):
    half = vector.shape[-1] // 2
    return jnp.concatenate([-vector[..., half:], vector[..., :half]], axis=-1)


def seq_begin(index, starts):
    return jnp.max(jnp.where(starts[None, :] <= index[:, None], starts[None, :], 0), axis=1)


def rope_tables(position, head):
    freq = jnp.exp(-math.log(10000.0) * jnp.arange(head // 2, dtype=jnp.float32) * (2.0 / head))
    angle = position[:, None] * freq[None, :]
    angle = jnp.concatenate([angle, angle], axis=1)
    return (jnp.cos(angle), jnp.sin(angle))


def dot32(left, right):
    return jnp.dot(left, right, preferred_element_type=jnp.float32)


def contract_rows(left, right):
    return lax.dot_general(
        left, right, (((0,), (0,)), ((), ())), preferred_element_type=jnp.float32
    )


def contract_cols(left, right):
    return lax.dot_general(
        left, right, (((1,), (1,)), ((), ())), preferred_element_type=jnp.float32
    )


def ffn_forward_fold(tokens_b, pieces):
    gate_rows, up_rows, down_rows = pieces
    gate_part = contract_cols(tokens_b, gate_rows)
    up_part = contract_cols(tokens_b, up_rows)
    gelu_value, gelu_slope = gelu_pair(gate_part)
    hidden = (gelu_value * up_part).astype(jnp.bfloat16)
    out_total = dot32(hidden, down_rows)
    return (out_total, gate_part, up_part)


def ffn_backward_fold(grad_b, gate_all, up_all, pieces):
    gate_rows, up_rows, down_rows = pieces
    hidden_grad = contract_cols(grad_b, down_rows)
    gelu_value, gelu_slope = gelu_pair(gate_all)
    dgate_b = (hidden_grad * up_all * gelu_slope).astype(jnp.bfloat16)
    dup_b = (hidden_grad * gelu_value).astype(jnp.bfloat16)
    in_total = dot32(dgate_b, gate_rows) + dot32(dup_b, up_rows)
    return (in_total, dgate_b, dup_b)


def ffn_weight_terms(tokens_b, grad_b, gate_all, up_all, dgate_all, dup_all):
    gelu_value, gelu_slope = gelu_pair(gate_all)
    hidden = (gelu_value * up_all).astype(jnp.bfloat16)
    return (
        contract_rows(dgate_all, tokens_b),
        contract_rows(dup_all, tokens_b),
        contract_rows(hidden, grad_b),
    )


def local(
    stream,
    stream_grad,
    lengths,
    w_qkv,
    w_out,
    w_gate,
    w_up,
    w_down,
    g_attn_in,
    g_query,
    g_key,
    g_attn_out,
    g_ffn_in,
    g_ffn_out,
):
    rows_in = stream[0]
    rows_grad = stream_grad[0]
    lens = lengths[0]
    rows = rows_in.shape[0]
    width = rows_in.shape[1]
    qwidth = HEADS * HEAD_DIM
    seq_count = lax.axis_size("seq")
    chip_bits = [2 * bit for bit in bits_of(lax.axis_size("dp") // 2)]
    seq_bits = bits_of(seq_count)
    nseq, nchip = len(seq_bits), len(chip_bits)
    seq_stages = [("seq", bit, nseq - 1 - k) for k, bit in enumerate(seq_bits)][::-1]
    chip_stages = [("dp", bit, nseq + nchip - 1 - k) for k, bit in enumerate(chip_bits)]
    core_stage = [("dp", 1, nseq + nchip)]
    all_up = seq_stages + chip_stages + core_stage
    all_down = seq_stages + chip_stages[::-1] + core_stage
    dp_count = lax.axis_size("dp")
    chips = dp_count // 2
    plane_up = [("dp", bit, nchip - 1 - k) for k, bit in enumerate(chip_bits)]
    plane_down = plane_up[::-1]
    cut = (width // 256) * 128 + (128 if width % 256 else 0)
    kv_stages = seq_stages
    keys = seq_count * rows
    scale = 1.0 / math.sqrt(HEAD_DIM)
    block_id = lax.axis_index("seq")
    dp_id = lax.axis_index("dp")
    seq_off = jnp.arange(seq_count, dtype=jnp.int32)
    chip_off = jnp.arange(chips, dtype=jnp.int32)
    core_off = jnp.arange(2, dtype=jnp.int32)
    qkv_own = w_qkv.shape[0]
    qkv_pad = (qkv_own + 8) // 8 * 8
    out_own = w_out.shape[0]
    ffn_own = w_gate.shape[0]
    half = w_qkv.shape[1] // 2
    qkv_dev = (
        (block_id ^ seq_off)[:, None, None] * dp_count
        + ((dp_id // 2) ^ chip_off)[None, :, None] * 2
        + ((dp_id % 2) ^ core_off)[None, None, :]
    ).reshape(-1, 1)
    lane = jnp.arange(qkv_pad, dtype=jnp.int32)[None, :]
    qkv_origin = jnp.where(lane < qkv_own, qkv_dev * qkv_own + lane, -1).reshape(-1)
    out_dev = qkv_dev
    out_origin = (out_dev * out_own + jnp.arange(out_own, dtype=jnp.int32)[None, :]).reshape(-1)
    qkv_order = one_hot_order(qkv_origin, width)
    out_order = one_hot_order(out_origin, qwidth)
    w_qkv_pad = jnp.pad(w_qkv, ((0, qkv_pad - qkv_own), (0, 0)))
    qkv_full = jnp.concatenate(
        [
            gather_xor(w_qkv_pad[:, :half], all_up),
            gather_xor(w_qkv_pad[:, half:], all_down),
        ],
        axis=-1,
    ).reshape(-1, 2 * half)
    out_full = gather_xor(w_out, all_down).reshape(-1, width)
    line_rows = lax.all_gather(
        jnp.concatenate([w_gate, w_up, w_down], axis=0),
        "seq",
        axis=0,
    )
    gate_full, up_full, down_full = (
        line_rows[:, i * ffn_own : (i + 1) * ffn_own].reshape(-1, width) for i in range(3)
    )
    starts = jnp.cumsum(lens) - lens
    own_index = block_id * rows + jnp.arange(rows, dtype=jnp.int32)
    key_index = (
        (block_id ^ jnp.arange(seq_count, dtype=jnp.int32))[:, None] * rows
        + jnp.arange(rows, dtype=jnp.int32)[None, :]
    ).reshape(keys)
    own_begin = seq_begin(own_index, starts)
    key_begin = seq_begin(key_index, starts)
    mask = (
        (key_begin[None, :] == own_begin[:, None])
        & (key_index[None, :] <= own_index[:, None])
        & (own_index[:, None] - key_index[None, :] < WINDOW)
    )
    full_mask = mask[:, None, :]
    cos_t, sin_t = rope_tables((own_index - own_begin).astype(jnp.float32), HEAD_DIM)
    root_attn = inv_root(rows_in)
    unit_attn = rows_in * root_attn
    attn_input = (unit_attn * g_attn_in).astype(jnp.bfloat16)
    attn_slots = dot32(attn_input, qkv_order).astype(jnp.bfloat16)
    projected = dot32(attn_slots, qkv_full)
    query = projected[:, :qwidth].reshape(rows, HEADS, HEAD_DIM)
    key_raw = projected[:, qwidth : qwidth + HEAD_DIM]
    value_raw = projected[:, qwidth + HEAD_DIM :]
    root_query = inv_root(query)
    unit_query = query * root_query
    query_norm = unit_query * g_query
    root_key = inv_root(key_raw)
    unit_key = key_raw * root_key
    key_norm = unit_key * g_key
    query_rot = query_norm * cos_t[:, None, :] + turn_half(query_norm) * sin_t[:, None, :]
    key_rot = key_norm * cos_t + turn_half(key_norm) * sin_t
    query_b = query_rot.astype(jnp.bfloat16)
    kv_own = jnp.concatenate([key_rot.astype(jnp.bfloat16), value_raw.astype(jnp.bfloat16)], axis=1)
    kv_all = gather_xor(kv_own, kv_stages).reshape(keys, 2 * HEAD_DIM)
    keys_b = kv_all[:, :HEAD_DIM]
    values_b = kv_all[:, HEAD_DIM:]
    scores = jnp.einsum("rhd,kd->rhk", query_b, keys_b, preferred_element_type=jnp.float32) * scale
    logsum = jnp.log(jnp.sum(jnp.where(full_mask, jnp.exp(scores), 0.0), axis=-1))
    probs = jnp.where(full_mask, jnp.exp(scores - logsum[..., None]), 0.0)
    probs_b = probs.astype(jnp.bfloat16)
    mixed = jnp.einsum("rhk,kd->rhd", probs_b, values_b, preferred_element_type=jnp.float32)
    mixed_b = mixed.reshape(rows, qwidth).astype(jnp.bfloat16)
    mixed_slots = dot32(mixed_b, out_order).astype(jnp.bfloat16)
    attn_out = dot32(mixed_slots, out_full)
    root_post = inv_root(attn_out)
    unit_post = attn_out * root_post
    hidden_in = rows_in + unit_post * g_attn_out
    root_ffn = inv_root(hidden_in)
    unit_ffn = hidden_in * root_ffn
    ffn_input = (unit_ffn * g_ffn_in).astype(jnp.bfloat16)

    def gather_tokens(value):
        both = jnp.concatenate(
            [gather_xor(value[:, :cut], plane_up), gather_xor(value[:, cut:], plane_down)], axis=-1
        )
        return mine_first(both[None], "dp", 1, 0).reshape(-1, width)

    def scatter_tokens(value):
        value = keep_half(value.reshape((2,) * (1 + nchip) + (rows, width)), "dp", 1, 0)[0]
        return jnp.concatenate(
            [
                scatter_xor(value[..., :cut], plane_down),
                scatter_xor(value[..., cut:], plane_up),
            ],
            axis=-1,
        )

    tokens_b = gather_tokens(ffn_input)
    out_part, gate_all, up_all = ffn_forward_fold(tokens_b, (gate_full, up_full, down_full))
    ffn_out = scatter_tokens(out_part)
    root_out = inv_root(ffn_out)
    unit_out = ffn_out * root_out
    result = hidden_in + unit_out * g_ffn_out
    grad_g_ffn_out = jnp.sum(rows_grad * unit_out, axis=0)
    ffn_grad_b = norm_back(rows_grad, unit_out, root_out, g_ffn_out).astype(jnp.bfloat16)
    grads_b = gather_tokens(ffn_grad_b)
    in_part, dgate_all, dup_all = ffn_backward_fold(
        grads_b, gate_all, up_all, (gate_full, up_full, down_full)
    )
    ffn_in_grad = scatter_tokens(in_part)
    terms = ffn_weight_terms(tokens_b, grads_b, gate_all, up_all, dgate_all, dup_all)
    ffn_in_grad, term_rows = lax.optimization_barrier(
        (
            ffn_in_grad,
            jnp.concatenate(
                [term.astype(jnp.bfloat16).reshape(seq_count, ffn_own, width) for term in terms],
                axis=1,
            ),
        )
    )
    ffn_terms = lax.psum_scatter(term_rows, "seq", scatter_dimension=0).astype(jnp.float32)
    ffn_terms = ffn_terms.reshape(3, ffn_own, width)
    grad_w_gate, grad_w_up, grad_w_down = ffn_terms[0], ffn_terms[1], ffn_terms[2]
    grad_g_ffn_in = jnp.sum(ffn_in_grad * unit_ffn, axis=0)
    hidden_grad_in = rows_grad + norm_back(ffn_in_grad, unit_ffn, root_ffn, g_ffn_in)
    grad_g_attn_out = jnp.sum(hidden_grad_in * unit_post, axis=0)
    attn_grad_b = norm_back(hidden_grad_in, unit_post, root_post, g_attn_out).astype(jnp.bfloat16)
    mixed_grad_slots = contract_cols(attn_grad_b, out_full).astype(jnp.bfloat16)
    mixed_grad_b = contract_cols(mixed_grad_slots, out_order).astype(jnp.bfloat16)
    spread = (2,) * (nseq + nchip + 1)
    out_term = contract_rows(mixed_slots, attn_grad_b).reshape(spread + w_out.shape)
    owned_out = scatter_xor(out_term, all_down[::-1])
    mixed_grad3 = mixed_grad_b.reshape(rows, HEADS, HEAD_DIM)
    delta = jnp.sum(
        mixed_grad3.astype(jnp.float32)
        * mixed_b.reshape(rows, HEADS, HEAD_DIM).astype(jnp.float32),
        axis=-1,
    )
    scores_again = (
        jnp.einsum("rhd,kd->rhk", query_b, keys_b, preferred_element_type=jnp.float32) * scale
    )
    probs_again = jnp.where(full_mask, jnp.exp(scores_again - logsum[..., None]), 0.0)
    probs_again_b = probs_again.astype(jnp.bfloat16)
    value_grad_all = jnp.einsum(
        "rhk,rhd->kd", probs_again_b, mixed_grad3, preferred_element_type=jnp.float32
    )
    prob_grad = jnp.einsum("rhd,kd->rhk", mixed_grad3, values_b, preferred_element_type=jnp.float32)
    score_grad_b = (probs_again * (prob_grad - delta[..., None])).astype(jnp.bfloat16)
    query_rot_grad = (
        jnp.einsum("rhk,kd->rhd", score_grad_b, keys_b, preferred_element_type=jnp.float32) * scale
    )
    key_grad_all = (
        jnp.einsum("rhk,rhd->kd", score_grad_b, query_b, preferred_element_type=jnp.float32) * scale
    )
    kv_grad_all = jnp.concatenate([key_grad_all, value_grad_all], axis=1)
    kv_grad = scatter_xor(
        kv_grad_all.reshape((2,) * nseq + (rows, 2 * HEAD_DIM)), kv_stages[::-1]
    )
    kv_grad, owned_out = lax.optimization_barrier((kv_grad, owned_out))
    key_rot_grad = kv_grad[:, :HEAD_DIM]
    value_grad = kv_grad[:, HEAD_DIM:]
    query_norm_grad = query_rot_grad * cos_t[:, None, :] - turn_half(
        query_rot_grad * sin_t[:, None, :]
    )
    key_norm_grad = key_rot_grad * cos_t - turn_half(key_rot_grad * sin_t)
    grad_g_query = jnp.sum(query_norm_grad * unit_query, axis=(0, 1))
    grad_g_key = jnp.sum(key_norm_grad * unit_key, axis=0)
    query_grad = norm_back(query_norm_grad, unit_query, root_query, g_query)
    key_grad = norm_back(key_norm_grad, unit_key, root_key, g_key)
    qkv_grad_b = jnp.concatenate(
        [query_grad.reshape(rows, qwidth), key_grad, value_grad], axis=1
    ).astype(jnp.bfloat16)
    attn_in_grad = in_order(contract_cols(qkv_grad_b, qkv_full), qkv_order)
    grad_g_attn_in = jnp.sum(attn_in_grad * unit_attn, axis=0)
    input_grad = hidden_grad_in + norm_back(attn_in_grad, unit_attn, root_attn, g_attn_in)
    spread = (2,) * (nseq + nchip + 1)
    count = seq_count * lax.axis_size("dp")
    gains = [grad_g_attn_in, grad_g_attn_out, grad_g_ffn_in, grad_g_ffn_out, grad_g_query, grad_g_key]
    gain_terms = jnp.concatenate([g.reshape(count, -1) for g in gains], axis=1)
    qkv_term = contract_rows(attn_slots, qkv_grad_b).reshape(spread + (qkv_pad, 2 * half))
    gain_slots = jnp.take(gain_terms, qkv_dev.reshape(-1), axis=0)
    left_term = qkv_term[..., :half].at[..., qkv_own, : gain_slots.shape[1]].set(
        gain_slots.reshape(spread + (-1,))
    )
    left_owned = scatter_xor(left_term, all_up[::-1])
    right_owned = scatter_xor(qkv_term[..., half:], all_down[::-1])
    owned_qkv = jnp.concatenate([left_owned, right_owned], axis=-1)[:qkv_own]
    owned = left_owned[qkv_own]
    own_width, own_head = width // count, HEAD_DIM // count
    owned_gains = [owned[i * own_width : (i + 1) * own_width] for i in range(4)]
    owned_heads = [
        owned[4 * own_width + i * own_head : 4 * own_width + (i + 1) * own_head] for i in range(2)
    ]
    return (
        result[None],
        input_grad[None],
        owned_qkv,
        owned_out,
        grad_w_gate,
        grad_w_up,
        grad_w_down,
        owned_gains[0],
        owned_heads[0],
        owned_heads[1],
        owned_gains[1],
        owned_gains[2],
        owned_gains[3],
    )


def solution(mesh):
    return jax.shard_map(
        local,
        mesh=mesh,
        in_specs=(
            P("dp", "seq", None),
            P("dp", "seq", None),
            P("dp", None),
            P(("seq", "dp"), None),
            P(("seq", "dp"), None),
            P(("seq", "dp"), None),
            P(("seq", "dp"), None),
            P(("seq", "dp"), None),
            P(),
            P(),
            P(),
            P(),
            P(),
            P(),
        ),
        out_specs=(
            P("dp", "seq", None),
            P("dp", "seq", None),
            P(("seq", "dp"), None),
            P(("seq", "dp"), None),
            P(("seq", "dp"), None),
            P(("seq", "dp"), None),
            P(("seq", "dp"), None),
            P(("seq", "dp")),
            P(("seq", "dp")),
            P(("seq", "dp")),
            P(("seq", "dp")),
            P(("seq", "dp")),
            P(("seq", "dp")),
        ),
        check_vma=False,
    )
```
